256 devices in a mesh: tm: 32 (over y, x, core), head: 8 (over z).
Axes of the slice: x: 4, y: 4, z: 8, core: 2. Of those that a mesh axis runs over, the one named last changes fastest.
Arguments:
- query_act: bfloat16 [8192, 3072], P('tm', 'head'), may hold values from -160 to 160
- key_act: bfloat16 [8192, 3072], P('tm', 'head'), may hold values from -7 to 7
- value_act: bfloat16 [8192, 3072], P('tm', 'head'), may hold values from -6 to 6
- d_output: bfloat16 [8192, 3072], P('tm', 'head'), may hold values from -6 to 6
- out_weight: bfloat16 [3072, 3072], P('head'), may hold values from -0.15625 to 0.15625
- block_mask: int32 [64, 64], P('tm'), may hold values from 0 to 1, as said below
Outputs:
- output: bfloat16 [8192, 3072], P('tm', 'head')
- d_query: bfloat16 [8192, 3072], P('tm', 'head')
- d_key: bfloat16 [8192, 3072], P('tm', 'head')
- d_value: bfloat16 [8192, 3072], P('tm', 'head')
The draws below stay inside these ranges and needn't reach their ends.
Inputs may be any that keep to these rules, and one draw needn't show every extreme that they name: With g(b) = b // 2 the frame group of block b: block_mask[a, b] is 1 whenever g(a) == g(b), and 0 unless |g(a) - g(b)| is 0, 1, 2, 3 or 4.
All inputs are finite; a program needn't handle non-finite values.
Results may differ from the reference program's by a relative error of at most 0.033.
Values may be sent and summed in bfloat16 or wider, within the bound.
No kernel may reach another device: no remote copies, remote signals or barrier semaphores. Data moves between devices by JAX's collectives and lax.ppermute only.
A program may use at most 64 MiB of HBM per device.

```python
import jax
import jax.numpy as jnp
from jax import lax

D = 3072
HEADS = 24
HEAD_DIM = 128
BLOCK = 128
TOK_DEV = 256
TOKENS = 8192
NBLK = 64
N_TM = 32


def shared_draw(key):
    base = jax.random.fold_in(key, 7)
    query_key, key_key = jax.random.split(base)
    queries = jnp.clip(jax.random.normal(query_key, (TOKENS, D), jnp.float32), -6.0, 6.0)
    keys_drawn = jnp.clip(jax.random.normal(key_key, (TOKENS, D), jnp.float32), -6.0, 6.0)
    return (queries, keys_drawn)


def draw_query_act(key, part):
    return shared_draw(key)[0].astype(jnp.bfloat16)


def draw_key_act(key, part):
    return shared_draw(key)[1].astype(jnp.bfloat16)


def draw_block_mask(key, part):
    per_group = TOK_DEV // BLOCK
    blocks = jnp.arange(NBLK)
    distance = jnp.abs(blocks[:, None] // per_group - blocks[None, :] // per_group)
    limit = jnp.where(distance == 0, 12, jnp.where(distance == 1, 6, jnp.where(distance <= 3, 4, jnp.where(distance == 4, 3, 0))))
    drawn = jax.random.randint(jax.random.fold_in(key, 11), (NBLK, NBLK), 0, 12)
    return (drawn < limit).astype(jnp.int32)


def spiked(entries, key, source, target, shards_of, factor):
    def block_of(position):
        return (jnp.arange(entries.shape[position]) // (entries.shape[position] // shards_of)).reshape((-1,) + (1,) * (entries.ndim - 1 - position))

    near = jax.random.permutation(key, shards_of)[block_of(target)]
    far = (block_of(target) + shards_of // 2) % shards_of
    return jnp.where((block_of(source) == near) | (block_of(source) == far), factor * entries, entries)


def steps_of(stream_key, shape, cuts, low, largest):
    factor_of = 1.0
    for axis_at, blocks in cuts:
        heights = jax.random.uniform(jax.random.fold_in(jax.random.fold_in(stream_key, 6), axis_at), (blocks,), jnp.float32, low / len(cuts), largest / len(cuts))
        factor_of = factor_of * jnp.repeat(jnp.exp(heights), shape[axis_at] // blocks).reshape((-1,) + (1,) * (len(shape) - 1 - axis_at))
    return factor_of


def centred(own_key, extent, scale, most, cuts=(), held_as=jnp.bfloat16):
    values = jax.random.normal(own_key, extent, jnp.float32) * scale
    if len(cuts) > 0:
        values = steps_of(own_key, extent, cuts, -0.22, 0.18) * values
    return jnp.clip(values, min=-most, max=most).astype(held_as)


def bell_draw_with(rng, extent, scale, reach, cuts, heavy, kind=jnp.bfloat16):
    values = scale * jax.random.normal(rng, extent, jnp.float32)
    if cuts:
        values = values * steps_of(rng, extent, cuts, -0.22, 0.18)
    return jnp.clip(spiked(values, jax.random.fold_in(rng, 3), *heavy), -reach, reach).astype(kind)


def setup_inputs(seed: int = 0) -> dict:
    key_list = jax.random.split(jax.random.key(seed), 7)
    return {
        "query_act": draw_query_act(jax.random.fold_in(key_list[6], 71), 0),
        "key_act": draw_key_act(jax.random.fold_in(key_list[6], 71), 0),
        "value_act": centred(key_list[2], (TOKENS, D), 1.0, 6.0, ((0, 32), (1, 8))),
        "d_output": centred(key_list[3], (TOKENS, D), 1.0, 6.0, ((0, 32), (1, 8))),
        "out_weight": bell_draw_with(key_list[4], (D, D), D ** -0.5, 0.15625, ((0, 8),), (0, 1, 8, 2.0)),
        "block_mask": draw_block_mask(jax.random.fold_in(key_list[6], 71), 0),
    }


def reference(query_act, key_act, value_act, d_output, out_weight, block_mask):
    score_scale = HEAD_DIM ** -0.5
    per_group = TOK_DEV // BLOCK
    margin = 4 * TOK_DEV
    span = 9 * TOK_DEV
    key_pad = jnp.pad(key_act, ((margin, margin), (0, 0)))
    value_pad = jnp.pad(value_act, ((margin, margin), (0, 0)))
    mask_pad = jnp.pad(block_mask, ((0, 0), (4 * per_group, 4 * per_group)))

    def group_probs(group):
        start = (group * TOK_DEV).astype(jnp.int32)
        q_rows = lax.dynamic_slice_in_dim(query_act, start, TOK_DEV, 0).astype(jnp.float32).reshape(TOK_DEV, HEADS, HEAD_DIM)
        k_rows = lax.dynamic_slice_in_dim(key_pad, start, span, 0).astype(jnp.float32).reshape(span, HEADS, HEAD_DIM)
        v_rows = lax.dynamic_slice_in_dim(value_pad, start, span, 0).astype(jnp.float32).reshape(span, HEADS, HEAD_DIM)
        block_start = (group * per_group).astype(jnp.int32)
        mask_rows = lax.dynamic_slice(mask_pad, (block_start, block_start), (per_group, 9 * per_group))
        allowed = jnp.repeat(jnp.repeat(mask_rows == 1, BLOCK, 0), BLOCK, 1)
        scores = jnp.einsum('thd,uhd->htu', q_rows, k_rows) * score_scale
        masked = jnp.where(allowed[None], scores, -jnp.inf)
        top = jnp.max(masked, axis=2, keepdims=True)
        expo = jnp.exp(masked - top)
        probs = expo / jnp.sum(expo, axis=2, keepdims=True)
        return q_rows, k_rows, v_rows, probs, start

    def forward_group(group):
        q_rows, k_rows, v_rows, probs, start = group_probs(group)
        weights = lax.optimization_barrier(probs.astype(jnp.bfloat16)).astype(jnp.float32)
        attn_rows = jnp.einsum('htu,uhd->thd', weights, v_rows)
        return attn_rows.reshape(TOK_DEV, D).astype(jnp.bfloat16)

    groups = jnp.arange(N_TM, dtype=jnp.int32)
    attn = lax.map(forward_group, groups).reshape(TOKENS, D)
    output = jnp.dot(attn, out_weight, preferred_element_type=jnp.float32).astype(jnp.bfloat16)
    d_attn = jnp.dot(d_output, out_weight.T, preferred_element_type=jnp.float32).astype(jnp.bfloat16)

    def backward_group(carry, group):
        dk_pad, dv_pad = carry
        q_rows, k_rows, v_rows, probs, start = group_probs(group)
        weights = lax.optimization_barrier(probs.astype(jnp.bfloat16)).astype(jnp.float32)
        grad_rows = lax.dynamic_slice_in_dim(d_attn, start, TOK_DEV, 0).astype(jnp.float32).reshape(TOK_DEV, HEADS, HEAD_DIM)
        attn_rows = lax.dynamic_slice_in_dim(attn, start, TOK_DEV, 0).astype(jnp.float32).reshape(TOK_DEV, HEADS, HEAD_DIM)
        delta = jnp.sum(grad_rows * attn_rows, axis=2).T[:, :, None]
        d_probs = jnp.einsum('thd,uhd->htu', grad_rows, v_rows)
        d_scores = lax.optimization_barrier((score_scale * probs * (d_probs - delta)).astype(jnp.bfloat16)).astype(jnp.float32)
        d_query_rows = jnp.einsum('htu,uhd->thd', d_scores, k_rows).reshape(TOK_DEV, D).astype(jnp.bfloat16)
        d_key_rows = jnp.einsum('htu,thd->uhd', d_scores, q_rows).reshape(span, D)
        d_value_rows = jnp.einsum('htu,thd->uhd', weights, grad_rows).reshape(span, D)
        dk_pad = lax.dynamic_update_slice_in_dim(dk_pad, lax.dynamic_slice_in_dim(dk_pad, start, span, 0) + d_key_rows, start, 0)
        dv_pad = lax.dynamic_update_slice_in_dim(dv_pad, lax.dynamic_slice_in_dim(dv_pad, start, span, 0) + d_value_rows, start, 0)
        return (dk_pad, dv_pad), d_query_rows

    zeros_pad = jnp.zeros((TOKENS + 2 * margin, D), jnp.float32)
    (dk_pad, dv_pad), d_query = lax.scan(backward_group, (zeros_pad, zeros_pad), groups)
    d_key = dk_pad[margin:margin + TOKENS].astype(jnp.bfloat16)
    d_value = dv_pad[margin:margin + TOKENS].astype(jnp.bfloat16)
    return output, d_query.reshape(TOKENS, D), d_key, d_value
```

```python
import functools

import jax
import jax.numpy as jnp
from jax import lax
from jax.experimental import pallas as pl
from jax.experimental.pallas import tpu as pltpu
from jax.sharding import PartitionSpec as P


HEAD_DIM = 128
BLOCK = 128
PARTS = 9
FAR = 3
BF16 = jnp.bfloat16
F32 = jnp.float32
VMEM_LIMIT = 40 * 1024 * 1024


def core_swap(value):
    count = lax.axis_size("tm")
    return lax.ppermute(value, "tm", [(s, s ^ 1) for s in range(count)])


def chip_step(value, sign):
    count = lax.axis_size("tm")
    pairs = [(s, (s + (2 * sign if s % 2 == 0 else -2 * sign)) % count) for s in range(count)]
    return lax.ppermute(value, "tm", pairs)


def ring_step(value):
    groups, count = lax.axis_size("tm"), lax.axis_size("head")
    pairs = [
        (t * count + z, t * count + (z + (1 if t % 2 == 0 else -1)) % count)
        for t in range(groups)
        for z in range(count)
    ]
    return lax.ppermute(value, ("tm", "head"), pairs)


def wide(x):
    return x.astype(F32)


def contract(left, right, left_dim, right_dim):
    return lax.dot_general(
        left, right, (((left_dim,), (right_dim,)), ((), ())), preferred_element_type=F32
    )


def place():
    tm = lax.axis_index("tm")
    core = lax.rem(tm, 2)
    return tm, core, lax.axis_index("head"), 1 - 2 * core


def part_groups():
    tm, core, _, way = place()
    chip = lax.div(tm, 2)
    back2, back1 = 2 * (chip - 2 * way), 2 * (chip - way)
    ahead2, ahead1 = 2 * (chip + 2 * way), 2 * (chip + way)
    other = 1 - core
    return [
        back2 + core,
        back2 + other,
        ahead2 + core,
        back1 + core,
        back1 + other,
        ahead1 + other,
        ahead1 + core,
        tm,
        2 * chip + other,
    ]


def pack_kernel(own_k, own_v, own_d, sib_k, sib_v, sib_d, kv_out, d_out, sems):
    rows = own_k.shape[0]
    copies = []
    for i, (source, target, at) in enumerate(
        (
            (own_k, kv_out, 0),
            (own_v, kv_out, 1),
            (sib_k, kv_out, 2),
            (sib_v, kv_out, 3),
            (own_d, d_out, 0),
            (sib_d, d_out, 1),
        )
    ):
        copies.append(
            pltpu.make_async_copy(source, target.at[pl.ds(at * rows, rows), :], sems.at[i])
        )
    for copy in copies:
        copy.start()
    for copy in copies:
        copy.wait()


def forward_kernel(scale, mask, query, r2, s2, r1, s1, both, weight_any, *refs):
    probs_out, attn_out, keep_out, send_out, mine_out, score_buf, attn_buf, weight, sem = refs
    head = pl.program_id(0)
    rows = query.shape[0]
    half = rows // 2
    cols = attn_buf.shape[1]
    blocks = rows // BLOCK
    count = weight.shape[1] // cols
    _, core, z, way = place()
    tm_count = lax.axis_size("tm")
    parts = [(r2, 0), (r2, 1), (s2, 0), (r1, 0), (r1, 1), (s1, 0), (s1, 1), (both, 0), (both, 1)]
    copy = pltpu.make_async_copy(weight_any, weight, sem)

    @pl.when(head == 0)
    def _():
        copy.start()

    q = query[...]
    top = None
    for p, ((part, at), group) in enumerate(zip(parts, part_groups())):
        inside = (group >= 0) & (group < tm_count)
        first = lax.clamp(0, group, tm_count - 1) * blocks
        keys = part[2 * at * rows : (2 * at + 1) * rows, :]
        scores = contract(keys, q, 1, 1) * scale
        for b in range(blocks):
            lanes = []
            for a in range(blocks):
                allowed = inside & (mask[a, first + b] == 1)
                lanes.append(jnp.full((1, BLOCK), jnp.where(allowed, 0.0, -jnp.inf), F32))
            piece = scores[b * BLOCK : (b + 1) * BLOCK] + jnp.concatenate(lanes, 1)
            score_buf[p * rows + b * BLOCK : p * rows + (b + 1) * BLOCK, :] = piece
            here = jnp.max(piece, axis=0, keepdims=True)
            top = here if top is None else jnp.maximum(top, here)
    total = None
    for p in range(PARTS):
        expo = jnp.exp(score_buf[p * rows : (p + 1) * rows, :] - top)
        score_buf[p * rows : (p + 1) * rows, :] = expo
        here = jnp.sum(expo, axis=0, keepdims=True)
        total = here if total is None else total + here
    inverse = 1.0 / total
    acc = None
    for p, (part, at) in enumerate(parts):
        weights = (score_buf[p * rows : (p + 1) * rows, :] * inverse).astype(BF16)
        probs_out[0, p * rows : (p + 1) * rows, :] = weights
        here = contract(part[(2 * at + 1) * rows : 2 * (at + 1) * rows, :], weights, 0, 0)
        acc = here if acc is None else acc + here
    attn_out[...] = acc.astype(BF16)
    attn_buf[:, pl.ds(pl.multiple_of(head * HEAD_DIM, HEAD_DIM), HEAD_DIM)] = acc.T.astype(BF16)

    @pl.when(head == pl.num_programs(0) - 1)
    def _():
        copy.wait()
        attn = attn_buf[...]

        def share(left, d):
            start = pl.multiple_of(lax.rem(z + d + count, count) * cols, HEAD_DIM)
            return contract(left, weight[:, pl.ds(start, cols)], 1, 0)

        mine_out[...] = share(attn, 0)
        for k in range(1, 4):
            keep_out[(k - 1) * rows : k * rows, :] = share(attn, way * k)
            send_out[(k - 1) * rows : k * rows, :] = share(attn, -way * k).astype(BF16)
        keep_rows = attn_buf[pl.ds(pl.multiple_of(core * half, half), half), :]
        send_rows = attn_buf[pl.ds(pl.multiple_of((1 - core) * half, half), half), :]
        keep_out[3 * rows :, :] = share(keep_rows, 4)
        send_out[3 * rows :, :] = share(send_rows, 4).astype(BF16)


def differentiate(scale, q, grad, attn, probs, parts):
    rows = q.shape[0]
    delta = jnp.sum(wide(grad).T * wide(attn), axis=0, keepdims=True)
    acc = None
    for p, (part, at, out, to) in enumerate(parts):
        keys, vals = 2 * at * rows, (2 * at + 1) * rows
        weights = probs[0, p * rows : (p + 1) * rows, :]
        out[(2 * to + 1) * rows : (2 * to + 2) * rows, :] = contract(weights, grad, 1, 0).astype(BF16)
        d_probs = contract(part[vals : vals + rows, :], grad, 1, 1)
        d_scores = (scale * wide(weights) * (d_probs - delta)).astype(BF16)
        out[2 * to * rows : (2 * to + 1) * rows, :] = contract(d_scores, q, 1, 0).astype(BF16)
        here = contract(part[keys : keys + rows, :], d_scores, 0, 0)
        acc = here if acc is None else acc + here
    return acc


def backward_far_kernel(scale, query, attn, probs, weight, r2, s2, *refs):
    own, a1, a2, a3, a4, b1, b2, b3, b4 = refs[:9]
    dq_out, grad_out, r2_out, s2_out, last = refs[9:]
    head = pl.program_id(0)
    rows, cols = grad_out.shape
    half = rows // 2
    count = weight.shape[1] // cols

    @pl.when(head == 0)
    def _():
        _, core, z, way = place()

        def term(piece, d):
            start = pl.multiple_of(lax.rem(z + d + count, count) * cols, HEAD_DIM)
            return contract(piece, weight[:, pl.ds(start, cols)], 1, 1)

        last[pl.ds(pl.multiple_of(core * half, half), half), :] = a4[:half, :]
        last[pl.ds(pl.multiple_of((1 - core) * half, half), half), :] = b4[...]
        acc = term(own[...], 0)
        for k, (a, b) in enumerate(((a1, b1), (a2, b2), (a3, b3))):
            acc += term(a[...], -way * (k + 1)) + term(b[...], way * (k + 1))
        acc += term(last[...], 4)
        grad_out[...] = acc.astype(BF16)

    grad = grad_out[:, pl.ds(pl.multiple_of(head * HEAD_DIM, HEAD_DIM), HEAD_DIM)]
    parts = [(r2, 0, r2_out, 0), (r2, 1, r2_out, 1), (s2, 0, s2_out, 0)]
    dq_out[...] = differentiate(scale, query[...], grad, attn[...], probs, parts)


def backward_near_kernel(scale, query, attn, probs, grad, dq_far, r1, s1, both, *refs):
    dq_out, r1_out, s1_out, both_out = refs
    parts = [(r, at, o, at) for r, o in ((r1, r1_out), (s1, s1_out), (both, both_out)) for at in (0, 1)]
    acc = differentiate(scale, query[...], grad[...], attn[...], probs, parts)
    dq_out[...] = (acc + dq_far[...]).T.astype(BF16)


def by_head(rows, at=0):
    return pl.BlockSpec((rows, HEAD_DIM), lambda h, *_: (at, h))


def by_head_rows(cols):
    return pl.BlockSpec((HEAD_DIM, cols), lambda h, *_: (h, 0))


def whole(rows, cols, at=0):
    return pl.BlockSpec((rows, cols), lambda h, *_: (at, 0))


def local(query_act, key_act, value_act, d_output, out_weight, block_mask):
    rows, cols = query_act.shape
    half = rows // 2
    scale = HEAD_DIM ** (-0.5)
    core = lax.axis_index("tm") % 2
    heads = cols // HEAD_DIM
    shape = jax.ShapeDtypeStruct
    vmem = pl.BlockSpec(memory_space=pltpu.VMEM)
    anywhere = pl.BlockSpec(memory_space=pl.ANY)
    limits = pltpu.CompilerParams(vmem_limit_bytes=VMEM_LIMIT)

    sib_k = core_swap(key_act)
    sib_v = core_swap(value_act)
    sib_d = core_swap(d_output)
    both, d_both = pl.pallas_call(
        pack_kernel,
        in_specs=[anywhere] * 6,
        out_specs=[vmem] * 2,
        out_shape=[shape((4 * rows, cols), BF16), shape((2 * rows, cols), BF16)],
        scratch_shapes=[pltpu.SemaphoreType.DMA((6,))],
        name="pack",
    )(key_act, value_act, d_output, sib_k, sib_v, sib_d)

    r1 = chip_step(both, 1)
    a1 = ring_step(d_both)
    a2 = ring_step(a1)
    r2 = chip_step(r1, 1)
    s1 = core_swap(r1)
    a3 = ring_step(a2)
    s2 = core_swap(r2)
    rest = jnp.where(
        core == 0,
        jnp.concatenate([a3[:half], a3[rows : rows + half]], 0),
        jnp.concatenate([a3[half:rows], a3[rows + half :]], 0),
    )
    a4 = ring_step(rest)
    b1 = core_swap(a1)
    b2 = core_swap(a2)
    b3 = core_swap(a3)
    b4 = core_swap(a4)

    probs, attn, keep, send, mine = pl.pallas_call(
        functools.partial(forward_kernel, scale),
        grid_spec=pltpu.PrefetchScalarGridSpec(
            num_scalar_prefetch=1,
            grid=(heads,),
            in_specs=[
                by_head(rows),
                by_head(4 * rows),
                by_head(2 * rows, 1),
                by_head(4 * rows),
                by_head(4 * rows),
                by_head(4 * rows),
                anywhere,
            ],
            out_specs=[
                pl.BlockSpec((1, PARTS * rows, rows), lambda h, *_: (h, 0, 0)),
                by_head_rows(rows),
                whole(3 * rows + half, cols),
                whole(3 * rows + half, cols),
                whole(rows, cols),
            ],
            scratch_shapes=[
                pltpu.VMEM((PARTS * rows, rows), F32),
                pltpu.VMEM((rows, cols), BF16),
                pltpu.VMEM(out_weight.shape, BF16),
                pltpu.SemaphoreType.DMA,
            ],
        ),
        out_shape=[
            shape((heads, PARTS * rows, rows), BF16),
            shape((cols, rows), BF16),
            shape((3 * rows + half, cols), F32),
            shape((3 * rows + half, cols), BF16),
            shape((rows, cols), F32),
        ],
        compiler_params=limits,
        cost_estimate=pl.CostEstimate(
            flops=4_000_000_000, bytes_accessed=12_000_000, transcendentals=1_800_000
        ),
        name="attend",
    )(block_mask, query_act, r2, s2, r1, s1, both, out_weight)

    other = core_swap(send)
    moved = ring_step(jnp.concatenate([keep[3 * rows :].astype(BF16), other[3 * rows :]], 0))
    in_half = (jnp.arange(rows) // half == core)[:, None]

    def spread(x):
        return jnp.where(in_half, jnp.concatenate([x, x], 0), 0.0)

    moved = jnp.concatenate([spread(wide(moved[:half])), spread(wide(moved[half:]))], 0)
    for k in (3, 2, 1):
        at = slice((k - 1) * rows, k * rows)
        moved = jnp.concatenate([keep[at] + moved[:rows], wide(other[at]) + moved[rows:]], 0)
        moved = wide(ring_step(moved.astype(BF16)))
    arrived = moved.astype(BF16)
    output = (mine + wide(arrived[:rows]) + wide(core_swap(arrived)[rows:])).astype(BF16)

    d_query_far, d_attn, g_r2, g_s2 = pl.pallas_call(
        functools.partial(backward_far_kernel, scale),
        grid=(heads,),
        in_specs=[
            by_head(rows),
            by_head_rows(rows),
            pl.BlockSpec((1, FAR * rows, rows), lambda h: (h, 0, 0)),
            whole(*out_weight.shape),
            by_head(4 * rows),
            by_head(2 * rows, 1),
        ]
        + [whole(rows, cols)] * 5
        + [whole(rows, cols, 1)] * 3
        + [whole(half, cols, 1)],
        out_specs=[by_head_rows(rows), whole(rows, cols), by_head(4 * rows), by_head(2 * rows)],
        out_shape=[
            shape((cols, rows), F32),
            shape((rows, cols), BF16),
            shape((4 * rows, cols), BF16),
            shape((2 * rows, cols), BF16),
        ],
        scratch_shapes=[pltpu.VMEM((rows, cols), BF16)],
        compiler_params=limits,
        cost_estimate=pl.CostEstimate(
            flops=2_500_000_000, bytes_accessed=8_000_000, transcendentals=0
        ),
        name="attend_back_far",
    )(query_act, attn, probs, out_weight, r2, s2, d_both, a1, a2, a3, a4, b1, b2, b3, b4)
    near = PARTS - FAR
    d_query, g_r1, g_s1, g_both = pl.pallas_call(
        functools.partial(backward_near_kernel, scale),
        grid=(heads,),
        in_specs=[
            by_head(rows),
            by_head_rows(rows),
            pl.BlockSpec(
                (pl.Element(1), pl.Element(near * rows), pl.Element(rows)),
                lambda h: (h, FAR * rows, 0),
            ),
            by_head(rows),
            by_head_rows(rows),
        ]
        + [by_head(4 * rows)] * 3,
        out_specs=[by_head(rows)] + [by_head(4 * rows)] * 3,
        out_shape=[shape((rows, cols), BF16)] + [shape((4 * rows, cols), BF16)] * 3,
        compiler_params=limits,
        cost_estimate=pl.CostEstimate(
            flops=4_000_000_000, bytes_accessed=10_000_000, transcendentals=0
        ),
        name="attend_back_near",
    )(query_act, attn, probs, d_attn, d_query_far, r1, s1, both)

    two = 2 * rows
    got = wide(core_swap(g_s2))
    back = jnp.concatenate([g_r2[:two], (wide(g_r2[two:]) + got).astype(BF16)], 0)
    back = chip_step(back, -1)
    back = (wide(g_r1) + wide(core_swap(g_s1)) + wide(back)).astype(BF16)
    back = chip_step(back, -1)
    over = core_swap((wide(g_both[two:]) + wide(back[two:])).astype(BF16))
    total = (wide(g_both[:two]) + wide(back[:two]) + wide(over)).astype(BF16)
    return (output, d_query, total[:rows], total[rows:])


def solution(mesh):
    placed = (
        P("tm", "head"),
        P("tm", "head"),
        P("tm", "head"),
        P("tm", "head"),
        P("head", None),
        P("tm", None),
    )
    return jax.shard_map(
        local,
        mesh=mesh,
        in_specs=placed,
        out_specs=(P("tm", "head"),) * 4,
        check_vma=False,
    )
```
